32 devices in a mesh: st: 8 (over y, x, core), tm: 4 (over z).
Axes of the slice: x: 2, y: 2, z: 4, core: 2. Of those that a mesh axis runs over, the one named last changes fastest.
Arguments:
- observed: float32 [8192, 2048], P('st', 'tm'), may hold values from -24 to 24
- station_xy: float32 [2, 8192], P(None, 'st'), may hold values from 0 to 33
- site_xy: float32 [2, 4096], P(None, 'st'), may hold values from 0 to 33
- time_points: float32 [2048], replicated, may hold values from 0 to 1, as said below
- pattern: int32 [64, 9], P('st'), may hold values from 0 to 63, as said below
- site_blocks: int32 [4096, 4], P('st'), may hold values from 0 to 63, as said below
Outputs:
- solution: float32 [8192, 2048], P('st', 'tm')
- predicted: float32 [4096, 2048], P('st', 'tm')
The draws below stay inside these ranges and needn't reach their ends.
Inputs may be any that keep to these rules, and one draw needn't show every extreme that they name: `pattern`: row b lists block b first, then blocks at most 4 away from b, one of them exactly 4 away. `site_blocks`: the home block of site j is j // 64; its list starts with the home block, then blocks at most 4 away from it, one of them exactly 4 away. `time_points`: column a holds a time between a / 2048 and (a + 1) / 2048.
All inputs are finite; a program needn't handle non-finite values.
Results may differ from the reference program's by a relative error of at most 0.0003.
Values sent between devices are 32-bit elements; how exact they have to be, the bound alone decides.
A program may use at most 128 MiB of HBM per device.

```python
import math
import jax
import jax.numpy as jnp
from jax import lax

BS = 128
REACH = 4
TREACH = 16
NNZ = 9
NNB = 4
SPB = 64
NT = 2048
ITERS = 2
NB = 64
STATIONS = 8192
NEW = 4096


def pick_blocks(key, home, count):
    row_count = home.shape[0]
    keys = jax.random.split(key, 2)
    side_sign = jax.random.randint(keys[0], (row_count,), 0, 2) * 2 - 1
    far_off = side_sign * REACH
    candidate = jnp.concatenate([jnp.arange(-REACH, 0, dtype=jnp.int32), jnp.arange(1, REACH + 1, dtype=jnp.int32)])
    scores = jax.random.randint(keys[1], (row_count, 2 * REACH), 0, 1 << 20) * (2 * REACH) + jnp.arange(2 * REACH, dtype=jnp.int32)[None, :]
    scores = jnp.where(candidate[None, :] == far_off[:, None], 1 << 30, scores)
    ranking = jnp.argsort(scores, axis=1)[:, :count - 2]
    others = candidate[ranking]
    offsets = jnp.concatenate([jnp.zeros((row_count, 1), jnp.int32), far_off[:, None].astype(jnp.int32), others.astype(jnp.int32)], axis=1)
    target = home[:, None] + offsets
    target = jnp.where((target < 0) | (target >= NB), home[:, None] - offsets, target)
    return target.astype(jnp.int32)


def draw_pattern(key, part):
    home = jnp.arange(NB, dtype=jnp.int32)
    return pick_blocks(jax.random.fold_in(key, 11), home, NNZ)


def draw_site_blocks(key, part):
    home = jnp.arange(NEW, dtype=jnp.int32) // SPB
    return pick_blocks(jax.random.fold_in(key, 13), home, NNB)


def draw_station_xy(key, part):
    block_pos = (jnp.arange(STATIONS) // BS).astype(jnp.float32)
    jitter = jax.random.uniform(key, (2, STATIONS), jnp.float32)
    return jnp.stack([0.5 * block_pos + jitter[0], jitter[1]]).astype(jnp.float32)


def draw_site_xy(key, part):
    block_pos = (jnp.arange(NEW) // SPB).astype(jnp.float32)
    jitter = jax.random.uniform(key, (2, NEW), jnp.float32)
    return jnp.stack([0.5 * block_pos + jitter[0], jitter[1]]).astype(jnp.float32)


def draw_time_points(key, part):
    jitter = jax.random.uniform(key, (NT,), jnp.float32)
    return ((jnp.arange(NT).astype(jnp.float32) + jitter) / NT).astype(jnp.float32)


def draw_observed(key, part):
    keys = jax.random.split(key, 1)
    rising = 1.0 + 2.0 * jnp.arange(STATIONS).astype(jnp.float32) / STATIONS
    base = jnp.clip(jax.random.normal(keys[0], (STATIONS, NT), jnp.float32), -6.0, 6.0)
    return (base * rising[:, None]).astype(jnp.float32)


def setup_inputs(seed: int = 0) -> dict:
    key_of = jax.random.split(jax.random.key(seed), 7)
    observed = draw_observed(jax.random.fold_in(key_of[6], 71), 0)
    station_xy = draw_station_xy(jax.random.fold_in(key_of[6], 71), 0)
    site_xy = draw_site_xy(jax.random.fold_in(key_of[6], 71), 0)
    time_points = draw_time_points(jax.random.fold_in(key_of[6], 71), 0)
    pattern = draw_pattern(jax.random.fold_in(key_of[6], 71), 0)
    site_blocks = draw_site_blocks(jax.random.fold_in(key_of[6], 71), 0)
    return dict(observed=observed, station_xy=station_xy, site_xy=site_xy, time_points=time_points, pattern=pattern, site_blocks=site_blocks)


HIGHEST_PREC = lax.Precision.HIGHEST
NUGGET = 1.0

def wendland(radius):
    remain = jnp.maximum(1.0 - radius, 0.0)
    return remain * remain * remain * remain * (4.0 * radius + 1.0)

def station_weight(diff_x, diff_y):
    return 2.5 / math.sqrt(NNZ * BS) * wendland(jnp.sqrt(diff_x * diff_x + diff_y * diff_y + 0.0001) / (0.75 * REACH))

def site_weight(diff_x, diff_y):
    return 2.5 / math.sqrt(NNB * BS) * wendland(jnp.sqrt(diff_x * diff_x + diff_y * diff_y + 0.0001) / (0.75 * REACH))

def reference(observed, station_xy, site_xy, time_points, pattern, site_blocks):
    time_kernel = 2.5 / math.sqrt(TREACH) * wendland(jnp.abs(time_points[:, None] - time_points[None, :]) * (NT / TREACH))
    blocks_xy = station_xy.reshape(2, NB, BS)
    row_xy = jnp.transpose(blocks_xy, (1, 0, 2))

    def space_apply(source):
        grouped = source.reshape(NB, BS, NT)

        def one_row(inputs):
            block_xy, block_ids = inputs
            partner = blocks_xy[:, block_ids]
            diff_x = block_xy[0][None, :, None] - partner[0][:, None, :]
            diff_y = block_xy[1][None, :, None] - partner[1][:, None, :]
            kernel_tiles = station_weight(diff_x, diff_y)
            return jnp.einsum('kij,kjt->it', kernel_tiles, grouped[block_ids], precision=HIGHEST_PREC)
        return lax.map(one_row, (row_xy, pattern)).reshape(NB * BS, NT)
    solution = jnp.zeros((NB * BS, NT), jnp.float32)
    resid = observed
    for sweep in range(ITERS):
        mixed = jnp.dot(resid, time_kernel, precision=HIGHEST_PREC)
        applied = space_apply(mixed) + NUGGET * resid
        inner_sum = jnp.sum(resid * applied)
        energy = jnp.sum(applied * applied)
        step_size = inner_sum / (energy + 1e-06)
        solution = solution + step_size * resid
        resid = resid - step_size * applied
    smoothed = jnp.dot(solution, time_kernel, precision=HIGHEST_PREC)
    margin = REACH * BS
    padded = jnp.pad(smoothed, ((margin, margin), (0, 0)))
    padded_xy = jnp.pad(station_xy, ((0, 0), (margin, margin)))
    window = (2 * REACH + 1) * BS
    group_xy = jnp.transpose(site_xy.reshape(2, NB, SPB), (1, 0, 2))
    group_blocks = site_blocks.reshape(NB, SPB, NNB)
    offsets = jnp.arange(2 * REACH + 1, dtype=jnp.int32)

    def one_group(inputs):
        home, own_xy, own_blocks = inputs
        first_row = (home * BS).astype(jnp.int32)
        near_rows = lax.dynamic_slice_in_dim(padded, first_row, window, 0)
        near_xy = lax.dynamic_slice_in_dim(padded_xy, first_row, window, 1)
        local_ids = own_blocks - home + REACH
        counts = lax.optimization_barrier(jnp.sum((local_ids[:, :, None] == offsets[None, None, :]).astype(jnp.float32), axis=1))
        diff_x = own_xy[0][:, None] - near_xy[0][None, :]
        diff_y = own_xy[1][:, None] - near_xy[1][None, :]
        weights = site_weight(diff_x, diff_y).reshape(SPB, 2 * REACH + 1, BS) * counts[:, :, None]
        return jnp.dot(weights.reshape(SPB, window), near_rows, precision=HIGHEST_PREC)
    predicted = lax.map(one_group, (jnp.arange(NB, dtype=jnp.int32), group_xy, group_blocks)).reshape(NB * SPB, NT)
    return (solution, predicted)
```

```python
import functools
import math

import jax
import jax.numpy as jnp
from jax import lax
from jax.experimental import pallas as pl
from jax.experimental.pallas import tpu as pltpu
from jax.sharding import PartitionSpec as P

BS = 128
REACH = 4
TREACH = 16
NNZ = 9
NNB = 4
NT = 2048
ITERS = 2
NUGGET = 1.0
MESH = pl.DeviceIdType.MESH
F32 = jnp.float32
BF16 = jnp.bfloat16


def wendland(radius):
    remain = jnp.maximum(1.0 - radius, 0.0)
    square = remain * remain
    return square * square * (4.0 * radius + 1.0)


def split(x):
    hi = x.astype(BF16)
    return hi, (x - hi.astype(F32)).astype(BF16)


def dot(a, b):
    return jnp.dot(a, b, preferred_element_type=F32)


def dot3(ah, al, bh, bl):
    return dot(ah, bh) + dot(ah, bl) + dot(al, bh)


def column(row):
    return jnp.transpose(jnp.broadcast_to(row, (BS, BS)))


def fold(x):
    rows, cols = x.shape
    x = jnp.sum(x.reshape(rows // 8, 8, cols), axis=0)
    total = x[:, :BS]
    for start in range(BS, cols, BS):
        total = total + x[:, start : start + BS]
    return total


def kernel(
    st_n,
    tm_n,
    obs,
    sxy,
    pxy,
    times,
    pattern,
    site_blocks,
    sol,
    pred,
    near,
    nx,
    ny,
    edge_out,
    edge_in,
    band_hi,
    band_lo,
    edge_band,
    pad,
    pad_hi,
    pad_lo,
    k_hi,
    k_lo,
    w_hi,
    w_lo,
    field,
    resid,
    pred_next,
    sums_tm,
    sums_st,
    xy_send,
    xy_recv,
    edge_send,
    edge_recv,
    pad_send,
    pad_recv,
    tm_send,
    tm_recv,
    st_send,
    st_recv,
):
    rows, width = obs.shape
    blocks = pattern.shape[0]
    groups = sxy.shape[0]
    sites = site_blocks.shape[0]
    margin = REACH * BS
    span = blocks + 2 * REACH
    chunk = 2 * BS
    pairs = blocks // 2
    lanes = width // BS
    st = lax.axis_index("st")
    tm = lax.axis_index("tm")
    has_low, has_high = st > 0, st < st_n - 1
    has_left, has_right = tm > 0, tm < tm_n - 1

    barrier = pltpu.get_barrier_semaphore()
    for d in range(1, st_n):
        pl.semaphore_signal(barrier, inc=1, device_id={"st": (st + d) % st_n}, device_id_type=MESH)
    for d in range(1, tm_n):
        pl.semaphore_signal(barrier, inc=1, device_id={"tm": (tm + d) % tm_n}, device_id_type=MESH)

    def shift(src, dst, send, recv, axis, pos, count, step):
        return pltpu.make_async_remote_copy(
            src_ref=src,
            dst_ref=dst,
            send_sem=send,
            recv_sem=recv,
            device_id={axis: (pos + step + count) % count},
            device_id_type=MESH,
        )

    def xy_copy(up):
        if up:
            return shift(sxy.at[groups - 1], near.at[0], xy_send.at[0], xy_recv.at[0], "st", st, st_n, 1)
        return shift(sxy.at[0], near.at[1], xy_send.at[1], xy_recv.at[1], "st", st, st_n, -1)

    def edge_copy(it, up):
        k = 1 if up else 0
        step = 1 if up else -1
        return shift(
            edge_out.at[it, k], edge_in.at[it, k], edge_send.at[it, k], edge_recv.at[it, k],
            "tm", tm, tm_n, step,
        )

    halves = margin // chunk

    def pad_copy(it, up, part):
        k = 1 if up else 0
        if up:
            source = margin + rows - margin + part * chunk
            target = part * chunk
        else:
            source = margin + part * chunk
            target = margin + rows + part * chunk
        return shift(
            pad.at[it, pl.ds(source, chunk)],
            pad.at[it, pl.ds(target, chunk)],
            pad_send.at[it, k, part],
            pad_recv.at[it, k, part],
            "st", st, st_n, 1 if up else -1,
        )

    def take_edges(source, it):
        for b in range(blocks):
            here = slice(b * BS, (b + 1) * BS)
            edge_out[it, 0, :, here] = jnp.transpose(source[here, :BS])[:TREACH]
            edge_out[it, 1, :, here] = jnp.transpose(source[here, width - BS :])[BS - TREACH :]

    def start_edges(it):
        @pl.when(has_left)
        def _():
            edge_copy(it, False).start()

        @pl.when(has_right)
        def _():
            edge_copy(it, True).start()

    def finish_edges(it):
        @pl.when(has_left)
        def _():
            edge_copy(it, True).wait_recv()

        @pl.when(has_right)
        def _():
            edge_copy(it, False).wait_recv()

        @pl.when(tm == 0)
        def _():
            edge_in[it, 1] = jnp.zeros_like(edge_in[it, 1])

        @pl.when(tm == tm_n - 1)
        def _():
            edge_in[it, 0] = jnp.zeros_like(edge_in[it, 0])

    def mix(source, it, left, right):
        def stack(x):
            hi, lo = split(x)
            return jnp.concatenate([hi, hi, lo], axis=0)

        for k, value in ((1, left), (0, right)):
            edges = stack(value)
            lane = 0 if k == 1 else width - BS
            for c in range(rows // chunk):
                here = pl.ds(margin + c * chunk, chunk)
                add = lax.dot_general(
                    edges[:, c * chunk : (c + 1) * chunk],
                    edge_band[k],
                    (((0,), (0,)), ((), ())),
                    preferred_element_type=F32,
                )
                pad[it, here, lane : lane + BS] = add
        order = []
        for part in range(halves):
            order.append((part, False, part))
            order.append((rows // chunk - halves + part, True, part))
        for c, up, part in order:
            hi, lo = split(source[c * chunk : (c + 1) * chunk, :])
            here = pl.ds(margin + c * chunk, chunk)
            mixed = dot3(hi, lo, band_hi[...], band_lo[...])
            first = mixed[:, :BS] + pad[it, here, :BS]
            last = mixed[:, width - BS :] + pad[it, here, width - BS :]
            mixed = jnp.concatenate([first, mixed[:, BS : width - BS], last], axis=1)
            pad[it, here, :] = mixed

            @pl.when(has_high if up else has_low)
            def _(up=up, part=part):
                pad_copy(it, up, part).start()

            pad_hi[it, here, :], pad_lo[it, here, :] = split(mixed)

    def receive(it, up, part):
        begin = part * chunk if up else margin + rows + part * chunk
        here = pl.ds(begin, chunk)

        @pl.when(has_low if up else has_high)
        def _():
            pad_copy(it, up, part).wait_recv()
            pad_hi[it, here, :], pad_lo[it, here, :] = split(pad[it, here, :])

        @pl.when(st == (0 if up else st_n - 1))
        def _():
            zero = jnp.zeros((chunk, width), BF16)
            pad_hi[it, here, :] = zero
            pad_lo[it, here, :] = zero

    half = min(width, 256)

    def apply_part(it, p, begin, end, col):
        here = slice(p * chunk, (p + 1) * chunk)
        cols = slice((begin - 2 * p) * BS, (end - 2 * p) * BS)
        ins = slice(begin * BS, end * BS)
        return dot3(
            k_hi[here, cols], k_lo[here, cols], pad_hi[it, ins, col], pad_lo[it, ins, col]
        )

    def apply_own(it):
        @pl.loop(0, width // half)
        def _(n):
            col = pl.ds(pl.multiple_of(n * half, half), half)
            for p in range(pairs):
                begin = max(2 * p, REACH)
                end = min(2 * p + 2 + 2 * REACH, REACH + blocks)
                field[p * chunk : (p + 1) * chunk, col] = apply_part(it, p, begin, end, col)

    def apply_halo(it, p, source):
        begin = max(2 * p, REACH)
        end = min(2 * p + 2 + 2 * REACH, REACH + blocks)
        here = slice(p * chunk, (p + 1) * chunk)
        inner = jnp.zeros((8, BS), F32)
        energy = jnp.zeros((8, BS), F32)
        for n in range(width // half):
            col = slice(n * half, (n + 1) * half)
            value = field[here, col]
            if 2 * p < begin:
                value = value + apply_part(it, p, 2 * p, begin, col)
            if end < 2 * p + 2 + 2 * REACH:
                value = value + apply_part(it, p, end, 2 * p + 2 + 2 * REACH, col)
            old = source[here, col]
            value = value + NUGGET * old
            field[here, col] = value
            inner = inner + fold(old * value)
            energy = energy + fold(value * value)
        return inner, energy

    def finish_apply(it, source):
        for part in range(halves):
            receive(it, True, part)
            receive(it, False, part)
        inner = jnp.zeros((8, BS), F32)
        energy = jnp.zeros((8, BS), F32)
        for p in range(pairs):
            one, two = apply_halo(it, p, source)
            inner, energy = inner + one, energy + two
        sums_tm[it, 0, :8] = inner
        sums_tm[it, 0, 8:] = energy

    def sum_copy(it, axis, d):
        if axis == "tm":
            return shift(sums_tm.at[it, 0], sums_tm.at[it, d], tm_send.at[it, d - 1],
                         tm_recv.at[it, d - 1], "tm", tm, tm_n, d)
        return shift(sums_st.at[it, 0], sums_st.at[it, d], st_send.at[it, d - 1],
                     st_recv.at[it, d - 1], "st", st, st_n, d)

    def start_sum(it, axis):
        for d in range(1, tm_n if axis == "tm" else st_n):
            sum_copy(it, axis, d).start()

    def finish_sum(it, axis):
        count, pos, buf = (tm_n, tm, sums_tm) if axis == "tm" else (st_n, st, sums_st)
        for d in range(1, count):
            sum_copy(it, axis, d).wait_recv()
        total = buf[it, pos % count]
        for j in range(1, count):
            total = total + buf[it, (pos - j + count) % count]
        return total

    def step_of(it):
        total = finish_sum(it, "st")
        inner = jnp.sum(jnp.sum(total[:8], axis=0, keepdims=True), axis=1, keepdims=True)
        energy = jnp.sum(jnp.sum(total[8:], axis=0, keepdims=True), axis=1, keepdims=True)
        return inner / (energy + 1e-06)

    take_edges(obs, 0)
    pl.semaphore_wait(barrier, st_n - 1 + tm_n - 1)
    start_edges(0)

    @pl.when(has_high)
    def _():
        xy_copy(True).start()

    @pl.when(has_low)
    def _():
        xy_copy(False).start()

    def time_row(i):
        count = times.shape[0]
        return times[pl.ds((tm * lanes + i + count) % count, 1), :]

    def time_tile(i, j):
        apart = jnp.abs(column(time_row(i)) - time_row(j))
        return 2.5 / math.sqrt(TREACH) * wendland(apart * (NT / TREACH))

    for i in range(lanes):
        for j in range(lanes):
            a = slice(i * BS, (i + 1) * BS)
            b = slice(j * BS, (j + 1) * BS)
            if abs(i - j) <= 1:
                band_hi[a, b], band_lo[a, b] = split(time_tile(i, j))
            else:
                band_hi[a, b] = jnp.zeros((BS, BS), BF16)
                band_lo[a, b] = jnp.zeros((BS, BS), BF16)
    for k, tile in (
        (1, time_tile(-1, 0)[BS - TREACH :]),
        (0, time_tile(lanes, lanes - 1)[:TREACH]),
    ):
        hi, lo = split(tile)
        edge_band[k] = jnp.concatenate([hi, lo, hi], axis=0)

    finish_edges(0)
    mix(obs, 0, edge_in[0, 1], edge_in[0, 0])

    @pl.when(has_low)
    def _():
        xy_copy(True).wait_recv()

    @pl.when(has_high)
    def _():
        xy_copy(False).wait_recv()

    @pl.when(st == 0)
    def _():
        near[0] = jnp.zeros_like(near[0])

    @pl.when(st == st_n - 1)
    def _():
        near[1] = jnp.zeros_like(near[1])

    for c, out in enumerate((nx, ny)):
        out[:REACH] = near[0, c]
        for g in range(groups):
            out[REACH * (g + 1) : REACH * (g + 2)] = sxy[g, c]
        out[REACH * (groups + 1) :] = near[1, c]

    lane_ids = lax.broadcasted_iota(jnp.int32, (BS, BS), 1)
    ids = pattern[...]
    k_counts = jnp.zeros((blocks, BS), F32)
    for s in range(NNZ):
        hit = ids[:, s : s + 1] == lane_ids[:blocks] + (st * blocks - REACH)
        k_counts = k_counts + hit.astype(F32)

    def weight(xcol, ycol, block, scale):
        dx = xcol - nx[pl.ds(block, 1), :]
        dy = ycol - ny[pl.ds(block, 1), :]
        radius = jnp.sqrt(dx * dx + dy * dy + 0.0001) * (1.0 / (0.75 * REACH))
        return scale * wendland(radius)

    for p in range(pairs):
        for q in range(2):
            b = 2 * p + q
            here = slice(b * BS, (b + 1) * BS)
            xcol = column(nx[REACH + b : REACH + b + 1, :])
            ycol = column(ny[REACH + b : REACH + b + 1, :])
            gap = (2 * REACH + 1 if q == 0 else 0) * BS
            k_hi[here, gap : gap + BS] = jnp.zeros((BS, BS), BF16)
            k_lo[here, gap : gap + BS] = jnp.zeros((BS, BS), BF16)
            for k in range(2 * REACH + 1):
                tile = weight(xcol, ycol, b + k, 2.5 / math.sqrt(NNZ * BS))
                tile = tile * k_counts[b : b + 1, b + k : b + k + 1]
                cols = slice((q + k) * BS, (q + k + 1) * BS)
                k_hi[here, cols], k_lo[here, cols] = split(tile)

    apply_own(0)
    finish_apply(0, obs)
    start_sum(0, "tm")
    take_edges(field, 1)
    start_edges(1)
    sums_st[0, 0] = finish_sum(0, "tm")
    start_sum(0, "st")

    site_rows = sites // pxy.shape[1]
    per_group = BS // (sites // blocks)
    wide = w_hi.shape[1] // BS
    site_chunks = pxy.shape[1]
    chunks_per = chunk // BS

    def site_tiles(h):
        here = slice(h * BS, (h + 1) * BS)
        base = (h // chunks_per) * chunks_per * per_group
        xcol = column(pxy[0, h : h + 1, :])
        ycol = column(pxy[1, h : h + 1, :])
        listed = site_blocks[here, :]
        counts = jnp.zeros((BS, BS), F32)
        for s in range(NNB):
            hit = listed[:, s : s + 1] == lane_ids + (st * blocks - REACH + base)
            counts = counts + hit.astype(F32)
        first = h * per_group - base
        for k in range(wide):
            cols = slice(k * BS, (k + 1) * BS)
            if first <= k < first + per_group + 2 * REACH:
                tile = weight(xcol, ycol, base + k, 2.5 / math.sqrt(NNB * BS))
                tile = tile * counts[:, k : k + 1]
                w_hi[here, cols], w_lo[here, cols] = split(tile)
            else:
                w_hi[here, cols] = jnp.zeros((BS, BS), BF16)
                w_lo[here, cols] = jnp.zeros((BS, BS), BF16)

    for h in range(site_chunks):
        site_tiles(h)

    finish_edges(1)
    step0 = step_of(0)
    for c in range(rows // chunk):
        here = slice(c * chunk, (c + 1) * chunk)
        resid[here, :] = obs[here, :] - step0 * field[here, :]
    mix(
        resid,
        1,
        edge_in[0, 1] - step0 * edge_in[1, 1],
        edge_in[0, 0] - step0 * edge_in[1, 0],
    )

    def predict(it, out):
        @pl.loop(0, width // half)
        def _(n):
            col = pl.ds(pl.multiple_of(n * half, half), half)
            for g in range(sites // chunk):
                here = slice(g * chunk, (g + 1) * chunk)
                base = g * chunks_per * per_group * BS
                ins = slice(base, base + wide * BS)
                out[here, col] = dot3(
                    w_hi[here, :], w_lo[here, :], pad_hi[it, ins, col], pad_lo[it, ins, col]
                )

    apply_own(1)
    predict(0, pred)
    finish_apply(1, resid)
    start_sum(1, "tm")
    sums_st[1, 0] = finish_sum(1, "tm")
    start_sum(1, "st")
    predict(1, pred_next)
    step1 = step_of(1)
    for c in range(rows // chunk):
        here = slice(c * chunk, (c + 1) * chunk)
        sol[here, :] = step0 * obs[here, :] + step1 * resid[here, :]
    for c in range(sites // chunk):
        here = slice(c * chunk, (c + 1) * chunk)
        pred[here, :] = step0 * pred[here, :] + step1 * pred_next[here, :]

    @pl.when(has_high)
    def _():
        xy_copy(True).wait_send()
        for it in range(ITERS):
            for part in range(halves):
                pad_copy(it, True, part).wait_send()

    @pl.when(has_low)
    def _():
        xy_copy(False).wait_send()
        for it in range(ITERS):
            for part in range(halves):
                pad_copy(it, False, part).wait_send()

    @pl.when(has_left)
    def _():
        for it in range(ITERS):
            edge_copy(it, False).wait_send()

    @pl.when(has_right)
    def _():
        for it in range(ITERS):
            edge_copy(it, True).wait_send()

    for it in range(ITERS):
        for axis, count in (("tm", tm_n), ("st", st_n)):
            for d in range(1, count):
                sum_copy(it, axis, d).wait_send()


def shards(st_n, tm_n, observed, station_xy, site_xy, time_points, pattern, site_blocks):
    rows, width = observed.shape
    blocks = pattern.shape[0]
    sites = site_blocks.shape[0]
    padded = rows + 2 * REACH * BS
    groups = blocks // REACH
    per_group = BS // (sites // blocks)
    wide = (2 * per_group + 2 * REACH) * BS
    halves = REACH // 2
    sxy = station_xy.reshape(2, groups, REACH, BS).transpose(1, 0, 2, 3)
    pxy = site_xy.reshape(2, sites // BS, BS)
    times = time_points.reshape(-1, BS)
    vmem = pl.BlockSpec(memory_space=pltpu.VMEM)
    dma = pltpu.SemaphoreType.DMA
    return pl.pallas_call(
        functools.partial(kernel, st_n, tm_n),
        out_shape=(
            jax.ShapeDtypeStruct((rows, width), F32),
            jax.ShapeDtypeStruct((sites, width), F32),
        ),
        in_specs=[vmem] * 6,
        out_specs=(vmem, vmem),
        scratch_shapes=[
            pltpu.VMEM((2, 2, REACH, BS), F32),
            pltpu.VMEM((blocks + 2 * REACH, BS), F32),
            pltpu.VMEM((blocks + 2 * REACH, BS), F32),
            pltpu.VMEM((ITERS, 2, TREACH, rows), F32),
            pltpu.VMEM((ITERS, 2, TREACH, rows), F32),
            pltpu.VMEM((width, width), BF16),
            pltpu.VMEM((width, width), BF16),
            pltpu.VMEM((2, 3 * TREACH, BS), BF16),
            pltpu.VMEM((ITERS, padded, width), F32),
            pltpu.VMEM((ITERS, padded, width), BF16),
            pltpu.VMEM((ITERS, padded, width), BF16),
            pltpu.VMEM((rows, (2 + 2 * REACH) * BS), BF16),
            pltpu.VMEM((rows, (2 + 2 * REACH) * BS), BF16),
            pltpu.VMEM((sites, wide), BF16),
            pltpu.VMEM((sites, wide), BF16),
            pltpu.VMEM((rows, width), F32),
            pltpu.VMEM((rows, width), F32),
            pltpu.VMEM((sites, width), F32),
            pltpu.VMEM((ITERS, tm_n, 16, BS), F32),
            pltpu.VMEM((ITERS, st_n, 16, BS), F32),
            dma((2,)),
            dma((2,)),
            dma((ITERS, 2)),
            dma((ITERS, 2)),
            dma((ITERS, 2, halves)),
            dma((ITERS, 2, halves)),
            dma((ITERS, tm_n - 1)),
            dma((ITERS, tm_n - 1)),
            dma((ITERS, st_n - 1)),
            dma((ITERS, st_n - 1)),
        ],
        compiler_params=pltpu.CompilerParams(
            collective_id=0, has_side_effects=True, vmem_limit_bytes=60 * 1024 * 1024
        ),
    )(observed, sxy, pxy, times, pattern, site_blocks)


def solution(mesh):
    placed = (P("st", "tm"), P(None, "st"), P(None, "st"), P(), P("st", None), P("st", None))
    return jax.shard_map(
        functools.partial(shards, mesh.shape["st"], mesh.shape["tm"]),
        mesh=mesh,
        in_specs=placed,
        out_specs=(P("st", "tm"), P("st", "tm")),
        check_vma=False,
    )
```

```python
import functools
import math

import jax
import jax.numpy as jnp
from jax import lax
from jax.experimental import pallas as pl
from jax.experimental.pallas import tpu as pltpu
from jax.sharding import PartitionSpec as P

BS = 128
REACH = 4
TREACH = 16
NNZ = 9
NNB = 4
NT = 2048
ITERS = 2
NUGGET = 1.0
MESH = pl.DeviceIdType.MESH
F32 = jnp.float32
BF16 = jnp.bfloat16


def wendland(radius, four, five):
    remain = jnp.maximum(1.0 - radius, 0.0)
    square = remain * remain
    return square * square * (five - four * remain)


def split(x):
    hi = x.astype(BF16)
    return hi, (x - hi.astype(F32)).astype(BF16)


def dot(a, b):
    return jnp.dot(a, b, preferred_element_type=F32)


def dot3(ah, al, bh, bl):
    return dot(ah, bh) + dot(ah, bl) + dot(al, bh)


def column(row):
    return jnp.transpose(jnp.broadcast_to(row, (BS, BS)))


def fold(x):
    rows, cols = x.shape
    x = jnp.sum(x.reshape(rows // 8, 8, cols), axis=0)
    total = x[:, :BS]
    for start in range(BS, cols, BS):
        total = total + x[:, start : start + BS]
    return total


def kernel(
    st_n,
    tm_n,
    obs,
    sxy,
    pxy,
    times,
    pattern,
    site_blocks,
    sol,
    pred,
    near,
    nx,
    ny,
    edge_out,
    edge_in,
    edge_parts,
    band_hi,
    band_lo,
    edge_band,
    halo,
    pad_hi,
    pad_lo,
    k_hi,
    k_lo,
    w_hi,
    w_lo,
    field,
    resid,
    pred_next,
    sums_tm,
    sums_st,
    xy_send,
    xy_recv,
    edge_send,
    edge_recv,
    halo_send,
    halo_recv,
    tm_send,
    tm_recv,
    st_send,
    st_recv,
):
    rows, width = obs.shape
    blocks = pattern.shape[0]
    sites = site_blocks.shape[1]
    margin = REACH * BS
    span = blocks + 2 * REACH
    chunk = 2 * BS
    pairs = blocks // 2
    lanes = width // BS
    st = lax.axis_index("st")
    tm = lax.axis_index("tm")
    has_low, has_high = st > 0, st < st_n - 1
    has_left, has_right = tm > 0, tm < tm_n - 1

    @pl.when(st == 0)
    def _():
        near[0] = jnp.zeros_like(near[0])
        for it in range(ITERS):
            halo[it, :margin] = jnp.zeros((margin, width), F32)

    @pl.when(st == st_n - 1)
    def _():
        near[1] = jnp.zeros_like(near[1])
        for it in range(ITERS):
            halo[it, margin:] = jnp.zeros((margin, width), F32)

    edge_in[...] = jnp.zeros_like(edge_in)

    barrier = pltpu.get_barrier_semaphore()
    for d in range(1, st_n):
        pl.semaphore_signal(barrier, inc=1, device_id={"st": (st + d) % st_n}, device_id_type=MESH)
    for d in range(1, tm_n):
        pl.semaphore_signal(barrier, inc=1, device_id={"tm": (tm + d) % tm_n}, device_id_type=MESH)
    for i in (st_n - 1, 1):
        for j in (tm_n - 1, 1):
            pl.semaphore_signal(
                barrier,
                inc=1,
                device_id={"st": (st + i) % st_n, "tm": (tm + j) % tm_n},
                device_id_type=MESH,
            )

    def shift(src, dst, send, recv, axis, pos, count, step):
        return pltpu.make_async_remote_copy(
            src_ref=src,
            dst_ref=dst,
            send_sem=send,
            recv_sem=recv,
            device_id={axis: (pos + step + count) % count},
            device_id_type=MESH,
        )

    def xy_copy(up):
        if up:
            return shift(sxy.at[:, pl.ds(rows - margin, margin)], near.at[0], xy_send.at[0],
                         xy_recv.at[0], "st", st, st_n, 1)
        return shift(sxy.at[:, pl.ds(0, margin)], near.at[1], xy_send.at[1], xy_recv.at[1],
                     "st", st, st_n, -1)

    def edge_copy(it, k, side):
        begin, count = ((0, rows), (rows - margin, margin), (0, margin))[side]
        target = (margin, 0, margin + rows)[side]
        to_tm = (tm + (1 if k else tm_n - 1)) % tm_n
        to_st = (st + (0, 1, st_n - 1)[side]) % st_n
        return pltpu.make_async_remote_copy(
            src_ref=edge_out.at[it, k, :, pl.ds(begin, count)],
            dst_ref=edge_in.at[it, k, :, pl.ds(target, count)],
            send_sem=edge_send.at[it, k, side],
            recv_sem=edge_recv.at[it, k, side],
            device_id={"st": to_st, "tm": to_tm},
            device_id_type=MESH,
        )

    send_tm = (has_left, has_right)
    recv_tm = (has_right, has_left)
    always = st >= 0
    send_st = (always, has_high, has_low)
    recv_st = (always, has_low, has_high)

    halves = margin // chunk

    def halo_copy(it, up, part):
        k = 1 if up else 0
        source = rows - margin + part * chunk if up else part * chunk
        target = part * chunk if up else margin + part * chunk
        origin = obs if it == 0 else field
        return shift(
            origin.at[pl.ds(source, chunk)],
            halo.at[it, pl.ds(target, chunk)],
            halo_send.at[it, k, part],
            halo_recv.at[it, k, part],
            "st", st, st_n, 1 if up else -1,
        )

    def start_halo(it, up, part):
        @pl.when(has_high if up else has_low)
        def _():
            halo_copy(it, up, part).start()

    def wait_halo(it, up, part):
        @pl.when(has_low if up else has_high)
        def _():
            halo_copy(it, up, part).wait_recv()

    def take_edges(source, it):
        for b in range(blocks):
            here = slice(b * BS, (b + 1) * BS)
            edge_out[it, 0, :, here] = jnp.transpose(source[here, :BS])[:TREACH]
            edge_out[it, 1, :, here] = jnp.transpose(source[here, width - BS :])[BS - TREACH :]

    def each_edge(send, action):
        tm_ok, st_ok = (send_tm, send_st) if send else (recv_tm, recv_st)
        for side in range(3):
            for k in range(2):
                @pl.when(jnp.logical_and(tm_ok[k], st_ok[side]))
                def _(k=k, side=side):
                    action(k, side)

    def start_edges(it):
        each_edge(True, lambda k, side: edge_copy(it, k, side).start())

    def finish_edges(it):
        each_edge(False, lambda k, side: edge_copy(it, k, side).wait_recv())

    def stack_edges(left, right):
        for k, value in ((1, left), (0, right)):
            hi, lo = split(value)
            edge_parts[k] = jnp.concatenate([hi, hi, lo], axis=0)

    def mix_rows(it, begin, value):
        hi, lo = split(value)
        mixed = dot3(hi, lo, band_hi[...], band_lo[...])
        sides = []
        for k in (1, 0):
            sides.append(lax.dot_general(
                edge_parts[k, :, begin : begin + chunk],
                edge_band[k],
                (((0,), (0,)), ((), ())),
                preferred_element_type=F32,
            ))
        mixed = jnp.concatenate(
            [mixed[:, :BS] + sides[0], mixed[:, BS : width - BS], mixed[:, width - BS :] + sides[1]],
            axis=1,
        )
        here = pl.ds(begin, chunk)
        pad_hi[it, here, :], pad_lo[it, here, :] = split(mixed)

    def mix_halo(it, step):
        for part in range(halves):
            for up in (True, False):
                wait_halo(it, up, part)
                first = part * chunk if up else margin + part * chunk
                here = pl.ds(first, chunk)
                value = halo[0, here, :]
                if it:
                    value = value - step * halo[1, here, :]
                mix_rows(it, first if up else first + rows, value)

    half = min(width, 256)

    def apply_part(it, p, begin, end, col):
        here = slice(p * chunk, (p + 1) * chunk)
        cols = slice((begin - 2 * p) * BS, (end - 2 * p) * BS)
        ins = slice(begin * BS, end * BS)
        return dot3(
            k_hi[here, cols], k_lo[here, cols], pad_hi[it, ins, col], pad_lo[it, ins, col]
        )

    fields = (field, sol)

    def apply_own(it):
        @pl.loop(0, width // half)
        def _(n):
            col = pl.ds(pl.multiple_of(n * half, half), half)
            for p in range(pairs):
                begin = max(2 * p, REACH)
                end = min(2 * p + 2 + 2 * REACH, REACH + blocks)
                fields[it][p * chunk : (p + 1) * chunk, col] = apply_part(it, p, begin, end, col)

    def apply_halo(it, p, source):
        begin = max(2 * p, REACH)
        end = min(2 * p + 2 + 2 * REACH, REACH + blocks)
        here = slice(p * chunk, (p + 1) * chunk)
        inner = jnp.zeros((8, BS), F32)
        energy = jnp.zeros((8, BS), F32)
        for n in range(width // half):
            col = slice(n * half, (n + 1) * half)
            value = fields[it][here, col]
            if 2 * p < begin:
                value = value + apply_part(it, p, 2 * p, begin, col)
            if end < 2 * p + 2 + 2 * REACH:
                value = value + apply_part(it, p, end, 2 * p + 2 + 2 * REACH, col)
            old = source[here, col]
            value = value + NUGGET * old
            fields[it][here, col] = value
            inner = inner + fold(old * value)
            energy = energy + fold(value * value)
        return inner, energy

    def finish_apply(it, source):
        inner = jnp.zeros((8, BS), F32)
        energy = jnp.zeros((8, BS), F32)
        for p in range(pairs):
            one, two = apply_halo(it, p, source)
            inner, energy = inner + one, energy + two
            if it == 0:
                if p < halves:
                    start_halo(1, False, p)
                if p >= pairs - halves:
                    start_halo(1, True, p - (pairs - halves))
        sums_tm[it, 0, :8] = inner
        sums_tm[it, 0, 8:] = energy

    def sum_copy(it, axis, d):
        if axis == "tm":
            return shift(sums_tm.at[it, 0], sums_tm.at[it, d], tm_send.at[it, d - 1],
                         tm_recv.at[it, d - 1], "tm", tm, tm_n, d)
        return shift(sums_st.at[it, 0], sums_st.at[it, d], st_send.at[it, d - 1],
                     st_recv.at[it, d - 1], "st", st, st_n, d)

    def start_sum(it, axis):
        for d in range(1, tm_n if axis == "tm" else st_n):
            sum_copy(it, axis, d).start()

    def finish_sum(it, axis):
        count, pos, buf = (tm_n, tm, sums_tm) if axis == "tm" else (st_n, st, sums_st)
        for d in range(1, count):
            sum_copy(it, axis, d).wait_recv()
        total = buf[it, pos % count]
        for j in range(1, count):
            total = total + buf[it, (pos - j + count) % count]
        return total

    def step_of(it):
        total = finish_sum(it, "st")
        inner = jnp.sum(jnp.sum(total[:8], axis=0, keepdims=True), axis=1, keepdims=True)
        energy = jnp.sum(jnp.sum(total[8:], axis=0, keepdims=True), axis=1, keepdims=True)
        return inner / (energy + 1e-06)

    take_edges(obs, 0)
    pl.semaphore_wait(barrier, st_n - 1 + tm_n - 1 + 4)
    start_edges(0)

    for part in range(halves):
        start_halo(0, False, part)
        start_halo(0, True, part)

    @pl.when(has_high)
    def _():
        xy_copy(True).start()

    @pl.when(has_low)
    def _():
        xy_copy(False).start()

    def time_row(i):
        count = times.shape[0]
        return times[pl.ds((tm * lanes + i + count) % count, 1), :]

    def time_tile(i, j):
        apart = jnp.abs(column(time_row(i)) - time_row(j))
        return wendland(apart * (NT / TREACH), 10.0 / math.sqrt(TREACH), 12.5 / math.sqrt(TREACH))

    for i in range(lanes):
        for j in range(lanes):
            a = slice(i * BS, (i + 1) * BS)
            b = slice(j * BS, (j + 1) * BS)
            if abs(i - j) <= 1:
                band_hi[a, b], band_lo[a, b] = split(time_tile(i, j))
            else:
                band_hi[a, b] = jnp.zeros((BS, BS), BF16)
                band_lo[a, b] = jnp.zeros((BS, BS), BF16)
    for k, tile in (
        (1, time_tile(-1, 0)[BS - TREACH :]),
        (0, time_tile(lanes, lanes - 1)[:TREACH]),
    ):
        hi, lo = split(tile)
        edge_band[k] = jnp.concatenate([hi, lo, hi], axis=0)

    finish_edges(0)
    stack_edges(edge_in[0, 1], edge_in[0, 0])
    for c in range(rows // chunk):
        mix_rows(0, margin + c * chunk, obs[c * chunk : (c + 1) * chunk, :])

    @pl.when(has_low)
    def _():
        xy_copy(True).wait_recv()

    @pl.when(has_high)
    def _():
        xy_copy(False).wait_recv()

    third = 1.0 / (0.75 * REACH)
    for c, out in enumerate((nx, ny)):
        for b in range(REACH):
            lane = slice(b * BS, (b + 1) * BS)
            out[b : b + 1, :] = near[0, c : c + 1, lane] * third
            high = REACH + blocks + b
            out[high : high + 1, :] = near[1, c : c + 1, lane] * third
        for b in range(blocks):
            out[REACH + b : REACH + b + 1, :] = sxy[c : c + 1, b * BS : (b + 1) * BS] * third

    lane_ids = lax.broadcasted_iota(jnp.int32, (BS, BS), 1)
    ids = pattern[...]
    k_counts = jnp.zeros((blocks, BS), F32)
    for s in range(NNZ):
        hit = ids[:, s : s + 1] == lane_ids[:blocks] + (st * blocks - REACH)
        k_counts = k_counts + hit.astype(F32)

    def weight(xcol, ycol, block, four, five):
        dx = xcol - nx[pl.ds(block, 1), :]
        dy = ycol - ny[pl.ds(block, 1), :]
        square = dx * dx + dy * dy + 0.0001 * third * third
        return wendland(square * lax.rsqrt(square), four, five)

    for p in range(pairs):
        for q in range(2):
            b = 2 * p + q
            here = slice(b * BS, (b + 1) * BS)
            xcol = column(nx[REACH + b : REACH + b + 1, :])
            ycol = column(ny[REACH + b : REACH + b + 1, :])
            gap = (2 * REACH + 1 if q == 0 else 0) * BS
            k_hi[here, gap : gap + BS] = jnp.zeros((BS, BS), BF16)
            k_lo[here, gap : gap + BS] = jnp.zeros((BS, BS), BF16)
            for k in range(2 * REACH + 1):
                count = jnp.broadcast_to(k_counts[b : b + 1, b + k : b + k + 1], (1, BS))
                unit = 2.5 / math.sqrt(NNZ * BS)
                tile = weight(xcol, ycol, b + k, count * (4.0 * unit), count * (5.0 * unit))
                cols = slice((q + k) * BS, (q + k + 1) * BS)
                k_hi[here, cols], k_lo[here, cols] = split(tile)

    apply_own(0)
    mix_halo(0, None)
    finish_apply(0, obs)
    start_sum(0, "tm")
    take_edges(field, 1)
    start_edges(1)
    sums_st[0, 0] = finish_sum(0, "tm")
    start_sum(0, "st")

    per_group = BS // (sites // blocks)
    wide = w_hi.shape[1] // BS
    site_chunks = sites // BS
    chunks_per = chunk // BS

    def site_tiles(h):
        here = slice(h * BS, (h + 1) * BS)
        base = (h // chunks_per) * chunks_per * per_group
        xcol = column(pxy[0:1, here] * third)
        ycol = column(pxy[1:2, here] * third)
        counts = jnp.zeros((BS, BS), F32)
        for s in range(NNB):
            listed = column((site_blocks[s : s + 1, here] - st * blocks).astype(F32))
            hit = listed == (lane_ids + (base - REACH)).astype(F32)
            counts = counts + hit.astype(F32)
        first = h * per_group - base
        for k in range(wide):
            cols = slice(k * BS, (k + 1) * BS)
            if first <= k < first + per_group + 2 * REACH:
                count = counts[:, k : k + 1]
                unit = 2.5 / math.sqrt(NNB * BS)
                tile = weight(xcol, ycol, base + k, count * (4.0 * unit), count * (5.0 * unit))
                w_hi[here, cols], w_lo[here, cols] = split(tile)
            else:
                w_hi[here, cols] = jnp.zeros((BS, BS), BF16)
                w_lo[here, cols] = jnp.zeros((BS, BS), BF16)

    for h in range(site_chunks):
        site_tiles(h)

    finish_edges(1)
    step0 = step_of(0)
    stack_edges(
        edge_in[0, 1] - step0 * edge_in[1, 1],
        edge_in[0, 0] - step0 * edge_in[1, 0],
    )
    for c in range(rows // chunk):
        here = slice(c * chunk, (c + 1) * chunk)
        value = obs[here, :] - step0 * field[here, :]
        resid[here, :] = value
        mix_rows(1, margin + c * chunk, value)

    def predict(it, out):
        @pl.loop(0, width // half)
        def _(n):
            col = pl.ds(pl.multiple_of(n * half, half), half)
            for g in range(sites // chunk):
                here = slice(g * chunk, (g + 1) * chunk)
                base = g * chunks_per * per_group * BS
                ins = slice(base, base + wide * BS)
                out[here, col] = dot3(
                    w_hi[here, :], w_lo[here, :], pad_hi[it, ins, col], pad_lo[it, ins, col]
                )

    apply_own(1)
    predict(0, pred)
    mix_halo(1, step0)
    finish_apply(1, resid)
    start_sum(1, "tm")
    sums_st[1, 0] = finish_sum(1, "tm")
    start_sum(1, "st")
    predict(1, pred_next)
    step1 = step_of(1)
    for c in range(rows // chunk):
        here = slice(c * chunk, (c + 1) * chunk)
        sol[here, :] = step0 * obs[here, :] + step1 * resid[here, :]
    for c in range(sites // chunk):
        here = slice(c * chunk, (c + 1) * chunk)
        pred[here, :] = step0 * pred[here, :] + step1 * pred_next[here, :]

    for up in (True, False):
        @pl.when(has_high if up else has_low)
        def _(up=up):
            xy_copy(up).wait_send()
            for part in range(halves):
                for it in range(ITERS):
                    halo_copy(it, up, part).wait_send()

    for it in range(ITERS):
        each_edge(True, lambda k, side: edge_copy(it, k, side).wait_send())

    for it in range(ITERS):
        for axis, count in (("tm", tm_n), ("st", st_n)):
            for d in range(1, count):
                sum_copy(it, axis, d).wait_send()


def shards(st_n, tm_n, observed, station_xy, site_xy, time_points, pattern, site_blocks):
    rows, width = observed.shape
    blocks = pattern.shape[0]
    sites = site_blocks.shape[0]
    padded = rows + 2 * REACH * BS
    per_group = BS // (sites // blocks)
    wide = (2 * per_group + 2 * REACH) * BS
    halves = REACH // 2
    times = time_points.reshape(-1, BS)
    vmem = pl.BlockSpec(memory_space=pltpu.VMEM)
    dma = pltpu.SemaphoreType.DMA
    return pl.pallas_call(
        functools.partial(kernel, st_n, tm_n),
        out_shape=(
            jax.ShapeDtypeStruct((rows, width), F32),
            jax.ShapeDtypeStruct((sites, width), F32),
        ),
        in_specs=[vmem] * 6,
        out_specs=(vmem, vmem),
        scratch_shapes=[
            pltpu.VMEM((2, 2, REACH * BS), F32),
            pltpu.VMEM((blocks + 2 * REACH, BS), F32),
            pltpu.VMEM((blocks + 2 * REACH, BS), F32),
            pltpu.VMEM((ITERS, 2, TREACH, rows), F32),
            pltpu.VMEM((ITERS, 2, TREACH, padded), F32),
            pltpu.VMEM((2, 3 * TREACH, padded), BF16),
            pltpu.VMEM((width, width), BF16),
            pltpu.VMEM((width, width), BF16),
            pltpu.VMEM((2, 3 * TREACH, BS), BF16),
            pltpu.VMEM((ITERS, 2 * REACH * BS, width), F32),
            pltpu.VMEM((ITERS, padded, width), BF16),
            pltpu.VMEM((ITERS, padded, width), BF16),
            pltpu.VMEM((rows, (2 + 2 * REACH) * BS), BF16),
            pltpu.VMEM((rows, (2 + 2 * REACH) * BS), BF16),
            pltpu.VMEM((sites, wide), BF16),
            pltpu.VMEM((sites, wide), BF16),
            pltpu.VMEM((rows, width), F32),
            pltpu.VMEM((rows, width), F32),
            pltpu.VMEM((sites, width), F32),
            pltpu.VMEM((ITERS, tm_n, 16, BS), F32),
            pltpu.VMEM((ITERS, st_n, 16, BS), F32),
            dma((2,)),
            dma((2,)),
            dma((ITERS, 2, 3)),
            dma((ITERS, 2, 3)),
            dma((ITERS, 2, halves)),
            dma((ITERS, 2, halves)),
            dma((ITERS, tm_n - 1)),
            dma((ITERS, tm_n - 1)),
            dma((ITERS, st_n - 1)),
            dma((ITERS, st_n - 1)),
        ],
        compiler_params=pltpu.CompilerParams(
            collective_id=0, has_side_effects=True, vmem_limit_bytes=60 * 1024 * 1024
        ),
    )(observed, station_xy, site_xy, times, pattern, site_blocks.T)


def solution(mesh):
    placed = (P("st", "tm"), P(None, "st"), P(None, "st"), P(), P("st", None), P("st", None))
    return jax.shard_map(
        functools.partial(shards, mesh.shape["st"], mesh.shape["tm"]),
        mesh=mesh,
        in_specs=placed,
        out_specs=(P("st", "tm"), P("st", "tm")),
        check_vma=False,
    )
```
